32 devices in a mesh: ex: 2 (over x), ey: 2 (over y), lin: 8 (over z, core).
Axes of the slice: x: 2, y: 2, z: 4, core: 2. Of those that a mesh axis runs over, the one named last changes fastest.
Arguments:
- load: float32 [5, 5, 5, 4, 16, 256], P(None, None, None, None, ('ey', 'lin'), 'ex'), may hold values from -6 to 6
- kappa: float32 [4, 16, 256], P(None, ('ey', 'lin'), 'ex'), may hold values from 0.3 to 3
- wet: int32 [4, 16, 256], P(None, ('ey', 'lin'), 'ex'), may hold values 0 or 1
Outputs:
- solution: float32 [5, 5, 5, 4, 16, 256], P(None, None, None, None, ('ey', 'lin'), 'ex')
- residual: float32 [5, 5, 5, 4, 16, 256], P(None, None, None, None, ('ey', 'lin'), 'ex')
The draws below stay inside these ranges and needn't reach their ends.
All inputs are finite; a program needn't handle non-finite values. No bound on the sum of `wet` on one device may be relied on, other than what follows from the above.
Results may differ from the reference program's by a relative error of at most 0.00016.
Values sent between devices are 32-bit elements; how exact they have to be, the bound alone decides.
A program may use at most 64 MiB of HBM per device.

```python
import math
import jax
import jax.numpy as jnp
import numpy as np
from jax import lax

LOBATTO_NODES = 5
ELEMENTS_DEPTH = 4
CYCLES = 2
NPRE = 2
NPOST = 2
NC = 4
ELEMENTS_ALONG = 256
ELEMENTS_ACROSS = 16


def set_ends(values, stream_key, low, top_value):
    shape = values.shape
    index_at = [jax.random.randint(jax.random.fold_in(stream_key, axis), (), 0, shape[axis]) for axis in range(len(shape))]
    values = values.at[tuple(index_at)].set(low)
    longest = shape.index(max(shape))
    index_at[longest] = (index_at[longest] + 1) % shape[longest]
    return values.at[tuple(index_at)].set(top_value)


def block_scale(key, extent, split, low, top_value):
    level, own = 1.0, jax.random.fold_in(key, 6)
    for position, shards_of in split:
        steps = jnp.exp(jax.random.uniform(jax.random.fold_in(own, position), (shards_of,), jnp.float32, low / len(split), top_value / len(split)))
        level = level * jnp.repeat(steps, extent[position] // shards_of).reshape([-1 if axis == position else 1 for axis in range(len(extent))])
    return level


def scatter_about(own_key, dims, deviation, bound, shards=(), kind=jnp.bfloat16):
    values = jax.random.normal(own_key, dims, jnp.float32) * deviation
    if len(shards) > 0:
        values = block_scale(own_key, dims, shards, -0.22, 0.18) * values
    return jnp.clip(values, min=-bound, max=bound).astype(kind)


def setup_inputs(seed: int = 0) -> dict:
    splits = jax.random.split(jax.random.key(seed), 4)
    load = scatter_about(splits[0], (LOBATTO_NODES, LOBATTO_NODES, LOBATTO_NODES, ELEMENTS_DEPTH, ELEMENTS_ACROSS, ELEMENTS_ALONG), 1.0, 6.0, ((4, 16), (5, 2)), jnp.float32)
    kappa = jnp.clip(jnp.exp(math.log(3.0) - 2.3025851 * jax.random.uniform(splits[1], (ELEMENTS_DEPTH, ELEMENTS_ACROSS, ELEMENTS_ALONG), jnp.float32) ** block_scale(splits[1], (ELEMENTS_DEPTH, ELEMENTS_ACROSS, ELEMENTS_ALONG), ((1, 16), (2, 2)), -0.2, 0.2)), 0.3, 3.0)
    wet = set_ends((jax.random.randint(splits[2], (ELEMENTS_DEPTH, ELEMENTS_ACROSS, ELEMENTS_ALONG), 0, 4) < 3).astype(jnp.int32), jax.random.fold_in(splits[2], 1), 0, 1)
    return dict(load=load, kappa=kappa, wet=wet)


fine_relax = 0.25
coarse_relax = 0.4

def node_tables():
    points = np.array([-1.0, -math.sqrt(3.0 / 7.0), 0.0, math.sqrt(3.0 / 7.0), 1.0])
    weights = np.array([0.1, 49.0 / 90.0, 32.0 / 45.0, 49.0 / 90.0, 0.1])
    eye_table = np.eye(points.shape[0])
    spread = points[:, None] - points[None, :] + eye_table
    factors = np.prod(spread, axis=1)
    deriv = factors[:, None] / (factors[None, :] * spread)
    deriv = np.where(eye_table > 0, (np.sum(1.0 / spread, axis=1) - 1.0)[:, None], deriv)
    stiff = deriv.T @ (weights[:, None] * deriv)
    mass = eye_table * weights[:, None]
    interp = np.stack([(1.0 - points) / 2.0, (1.0 + points) / 2.0], axis=1)
    coarse_stiff = interp.T @ stiff @ interp
    coarse_mass = interp.T @ mass @ interp
    return [jnp.asarray(table, jnp.float32) for table in (stiff, mass, interp, coarse_stiff, coarse_mass)]

def along(matrix, field, axis):
    if axis == 0:
        return jnp.einsum('pa,a...->p...', matrix, field, precision=lax.Precision.HIGHEST)
    if axis == 1:
        return jnp.einsum('qb,ab...->aq...', matrix, field, precision=lax.Precision.HIGHEST)
    return jnp.einsum('rc,abc...->abr...', matrix, field, precision=lax.Precision.HIGHEST)

def element_apply(field, coeff, stiff, mass):
    mass_c = along(mass, field, 2)
    mass_bc = along(mass, mass_c, 1)
    first_term = along(stiff, mass_bc, 0)
    second_term = along(mass, along(stiff, mass_c, 1), 0)
    third_term = along(mass, along(mass, along(stiff, field, 2), 1), 0)
    return coeff * (first_term + second_term + third_term)

def element_diagonal(coeff, stiff, mass):
    stiff_diag = jnp.diagonal(stiff)
    mass_diag = jnp.diagonal(mass)
    local = stiff_diag[:, None, None] * mass_diag[None, :, None] * mass_diag[None, None, :] + mass_diag[:, None, None] * stiff_diag[None, :, None] * mass_diag[None, None, :] + mass_diag[:, None, None] * mass_diag[None, :, None] * stiff_diag[None, None, :]
    return local[:, :, :, None, None, None] * coeff[None, None, None]

def pair_sum(field, node_axis, fetch):
    count = field.shape[node_axis]
    lower = lax.index_in_dim(field, 0, node_axis, keepdims=False)
    upper = lax.index_in_dim(field, count - 1, node_axis, keepdims=False)
    elem_axis = node_axis + 2
    length = lower.shape[elem_axis]
    lower_first = lax.slice_in_dim(lower, 0, 1, axis=elem_axis)
    upper_last = lax.slice_in_dim(upper, length - 1, length, axis=elem_axis)
    outer = fetch(jnp.concatenate([lower_first, upper_last], axis=elem_axis))
    inner = lax.slice_in_dim(upper, 0, length - 1, axis=elem_axis) + lax.slice_in_dim(lower, 1, length, axis=elem_axis)
    head = lower_first + lax.slice_in_dim(outer, 0, 1, axis=elem_axis)
    tail = upper_last + lax.slice_in_dim(outer, 3, 4, axis=elem_axis)
    new_lower = jnp.concatenate([head, inner], axis=elem_axis)
    new_upper = jnp.concatenate([inner, tail], axis=elem_axis)
    middle = lax.slice_in_dim(field, 1, count - 1, axis=node_axis)
    return jnp.concatenate([jnp.expand_dims(new_lower, node_axis), middle, jnp.expand_dims(new_upper, node_axis)], axis=node_axis)

def pad_edge(axis):

    def padded(edge):
        widths = [(1, 1) if dim == axis else (0, 0) for dim in range(edge.ndim)]
        return jnp.pad(edge, widths)
    return padded

def assemble(field, fetch_x, fetch_y, fetch_z):
    field = pair_sum(field, 2, fetch_x)
    field = pair_sum(field, 1, fetch_y)
    return pair_sum(field, 0, fetch_z)

def surface_mask(count, layers, offset, total):
    node = jnp.arange(count, dtype=jnp.int32)[:, None]
    layer = jnp.arange(layers, dtype=jnp.int32)[None, :] + offset
    keep = jnp.where((node == count - 1) & (layer == total - 1), jnp.float32(0.0), jnp.float32(1.0))
    return keep.reshape(count, 1, 1, layers, 1, 1)

def coarse_sweeps(local, coeff, coarse_sum, keep, inverse, coarse_stiff, coarse_mass):
    restricted = keep * coarse_sum(local)
    correction = inverse * restricted
    for sweep in range(NC - 1):
        image = keep * coarse_sum(element_apply(correction, coeff, coarse_stiff, coarse_mass))
        correction = correction + inverse * (restricted - image)
    return correction

def multigrid(load, coeff, fine_sum, keep, coarse_correct, tables):
    stiff, mass, interp, coarse_stiff, coarse_mass = tables
    inverse = fine_relax / fine_sum(element_diagonal(coeff, stiff, mass))
    rhs = keep * fine_sum(load)
    solution = jnp.zeros_like(load)

    def sweep_once(solution):
        change = keep * fine_sum(load - element_apply(solution, coeff, stiff, mass))
        return solution + inverse * change
    transpose = interp.T
    for cycle in range(CYCLES):
        for sweep in range(NPRE):
            if cycle == 0 and sweep == 0:
                solution = solution + inverse * rhs
            else:
                solution = sweep_once(solution)
        local = load - element_apply(solution, coeff, stiff, mass)
        local = along(transpose, along(transpose, along(transpose, local, 2), 1), 0)
        correction = coarse_correct(local)
        solution = solution + along(interp, along(interp, along(interp, correction, 2), 1), 0)
        for sweep in range(NPOST):
            solution = sweep_once(solution)
    residual = keep * fine_sum(load - element_apply(solution, coeff, stiff, mass))
    return (solution, residual)

def reference(load, kappa, wet):
    tables = node_tables()
    stiff, mass, interp, coarse_stiff, coarse_mass = tables
    coeff = kappa * jnp.where(wet == 1, jnp.float32(1.0), jnp.float32(0.05))

    def whole_sum(field):
        return assemble(field, pad_edge(4), pad_edge(3), pad_edge(2))
    fine_retain_mask = surface_mask(LOBATTO_NODES, ELEMENTS_DEPTH, 0, ELEMENTS_DEPTH)
    coarse_retain_mask = surface_mask(2, ELEMENTS_DEPTH, 0, ELEMENTS_DEPTH)
    coarse_inverse = coarse_relax / whole_sum(element_diagonal(coeff, coarse_stiff, coarse_mass))

    def coarse_correct(local):
        return coarse_sweeps(local, coeff, whole_sum, coarse_retain_mask, coarse_inverse, coarse_stiff, coarse_mass)
    return multigrid(load, coeff, whole_sum, fine_retain_mask, coarse_correct, tables)
```

```python
import functools
import math

import jax
import jax.numpy as jnp
import numpy as np
from jax import lax
from jax.experimental import pallas as pl
from jax.experimental.pallas import tpu as pltpu
from jax.sharding import PartitionSpec as P

N = 5
CYCLES = 2
NPRE = 2
NPOST = 2
NC = 4
FINE_RELAX = 0.25
COARSE_RELAX = 0.4
REACH = NC
STEPS = CYCLES * (NPRE + NPOST) + 1
HALO = 32
MESH = pl.DeviceIdType.MESH
F32 = jnp.float32


def node_tables():
    points = np.array([-1.0, -math.sqrt(3.0 / 7.0), 0.0, math.sqrt(3.0 / 7.0), 1.0])
    weights = np.array([0.1, 49.0 / 90.0, 32.0 / 45.0, 49.0 / 90.0, 0.1])
    eye_table = np.eye(points.shape[0])
    spread = points[:, None] - points[None, :] + eye_table
    factors = np.prod(spread, axis=1)
    deriv = factors[:, None] / (factors[None, :] * spread)
    deriv = np.where(eye_table > 0, (np.sum(1.0 / spread, axis=1) - 1.0)[:, None], deriv)
    stiff = deriv.T @ (weights[:, None] * deriv)
    mass = eye_table * weights[:, None]
    interp = np.stack([(1.0 - points) / 2.0, (1.0 + points) / 2.0], axis=1)
    return stiff, weights, interp, interp.T @ stiff @ interp, interp.T @ mass @ interp


STIFF, WEIGHTS, INTERP, COARSE_STIFF, COARSE_MASS = node_tables()
D = STIFF / WEIGHTS[:, None]
W3 = WEIGHTS[:, None, None] * WEIGHTS[None, :, None] * WEIGHTS[None, None, :]
DD = np.diag(D)
K3 = W3 * (DD[:, None, None] + DD[None, :, None] + DD[None, None, :])


def node(a, b, c):
    return (a * N + b) * N + c


def line_parts(v):
    twice = v[2] + v[2]
    return (v[0] + v[4]) - twice, (v[1] + v[3]) - twice, v[0] - v[4], v[1] - v[3]


def row_even(i, parts):
    return float((D[i, 0] + D[i, 4]) / 2) * parts[0] + float((D[i, 1] + D[i, 3]) / 2) * parts[1]


def row_odd(i, parts):
    return float((D[i, 0] - D[i, 4]) / 2) * parts[2] + float((D[i, 1] - D[i, 3]) / 2) * parts[3]


def line_apply(v):
    parts = line_parts(v)
    e0, e1, e2 = (row_even(i, parts) for i in range(3))
    o0, o1 = (row_odd(i, parts) for i in range(2))
    return [e0 + o0, e1 + o1, e2, e1 - o1, e0 - o0]


def scaled(factor, value):
    factor = float(factor)
    if factor == 1.0:
        return value
    return factor * value


def mix(pairs):
    total = None
    for factor, value in pairs:
        if abs(float(factor)) < 1e-14:
            continue
        term = scaled(factor, value)
        total = term if total is None else total + term
    return total


def kernel(
    sizes, load_ref, kappa_ref, wet_ref, sol_out, res_out,
    other_load, other_coeff, own_coeff, load, coeffs, sol, total, inverse, cinv, face, got, cgot,
    ex_send, ex_recv, k_send, k_recv, f_send, f_recv, c_send, c_recv,
):
    ex_count, ey_count, lin_count, layers, width = sizes
    ex, ey, lin = lax.axis_index("ex"), lax.axis_index("ey"), lax.axis_index("lin")
    rows = ey_count * lin_count
    row = ey * lin_count + lin
    own = REACH

    sub = lax.broadcasted_iota(jnp.int32, (2 * layers, width), 0)
    lane = lax.broadcasted_iota(jnp.int32, (2 * layers, width), 1)
    layer = sub % layers
    bottom, top = layer == 0, layer == layers - 1
    first_lane, last_lane = lane == 0, lane == width - 1
    near = jnp.where(ex == 0, lane, width - 1 - lane)
    real = (sub < layers) | (near < HALO)

    def like(mask, x):
        return jnp.broadcast_to(mask, x.shape) if x.ndim == 3 else mask

    def before(x):
        y = pltpu.roll(x, 1, x.ndim - 1)
        return jnp.where(like(first_lane, x), pltpu.roll(y, layers, x.ndim - 2), y)

    def after(x):
        y = pltpu.roll(x, width - 1, x.ndim - 1)
        return jnp.where(like(last_lane, x), pltpu.roll(y, layers, x.ndim - 2), y)

    def below(low, high):
        return jnp.where(like(bottom, low), low, low + pltpu.roll(high, 1, low.ndim - 2))

    def above(low):
        return jnp.where(like(top, low), 0.0, pltpu.roll(low, 2 * layers - 1, low.ndim - 2))

    def place(at):
        return (ex, at // lin_count, at % lin_count)

    def partners(fn):
        for d in range(1, REACH + 1):
            @pl.when(row >= d)
            def _():
                fn(row - d, own + d, own - d)

            @pl.when(row + d < rows)
            def _():
                fn(row + d, own - d, own + d)

    coeffs[...] = jnp.zeros_like(coeffs)
    cgot[...] = jnp.zeros_like(cgot)
    got[...] = jnp.zeros_like(got)
    barrier = pltpu.get_barrier_semaphore()
    pl.semaphore_signal(barrier, inc=1, device_id=(1 - ex, ey, lin), device_id_type=MESH)
    partners(lambda at, theirs, mine: pl.semaphore_signal(
        barrier, inc=1, device_id=place(at), device_id_type=MESH))

    coeff_own = kappa_ref[...] * jnp.where(wet_ref[...] == 1, F32(1.0), F32(0.05))
    own_coeff[...] = coeff_own

    pl.semaphore_wait(barrier, 1 + jnp.minimum(row, REACH) + jnp.minimum(rows - 1 - row, REACH))

    def ex_copy(src, dst, i):
        return pltpu.make_async_remote_copy(
            src_ref=src, dst_ref=dst, send_sem=ex_send.at[i], recv_sem=ex_recv.at[i],
            device_id=(1 - ex, ey, lin), device_id_type=MESH)

    coeff_copy = ex_copy(own_coeff, other_coeff, 0)
    load_copy = ex_copy(load_ref, other_load, 1)
    coeff_copy.start()
    load_copy.start()
    sol[...] = jnp.zeros_like(sol)
    coeff_copy.wait()
    coeffs[own] = jnp.where(real, jnp.concatenate([coeff_own, other_coeff[...]], axis=0), 0.0)

    def k_copy(at, theirs, mine):
        return pltpu.make_async_remote_copy(
            src_ref=coeffs.at[own], dst_ref=coeffs.at[theirs],
            send_sem=k_send.at[mine], recv_sem=k_recv.at[theirs],
            device_id=place(at), device_id_type=MESH)

    def k_wait(at, theirs, mine):
        pltpu.make_async_remote_copy(
            src_ref=coeffs.at[own], dst_ref=coeffs.at[mine],
            send_sem=k_send.at[mine], recv_sem=k_recv.at[mine],
            device_id=place(at), device_id_type=MESH).wait()

    partners(lambda *p: k_copy(*p).start())
    load_copy.wait()

    def join(i, _):
        load[i] = jnp.where(real, jnp.concatenate([load_ref[i], other_load[i]], axis=0), 0.0)
        return 0

    lax.fori_loop(0, N * N * N, join, 0)
    partners(k_wait)

    def inverted(x):
        return jnp.where(x > 0.0, 1.0 / jnp.where(x > 0.0, x, 1.0), 0.0)

    here = coeffs[own]
    for kind, x in enumerate((here, here + coeffs[own - 1], here + coeffs[own + 1])):
        xc = x + before(x)
        for slot, y in enumerate((x, xc, below(x, x), below(xc, xc))):
            inverse[kind * 4 + slot] = inverted(y)
    pairs = coeffs[0:2 * REACH] + coeffs[1:2 * REACH + 1]
    pairs = pairs + before(pairs)
    pairs = below(pairs, pairs)
    corner = 3.0 * COARSE_STIFF[0, 0] * COARSE_MASS[0, 0] ** 2
    cinv[...] = float(COARSE_RELAX / corner) * inverted(pairs)

    def plane_local(b):
        v = [[sol[node(a, b, c)] for c in range(N)] for a in range(N)]
        acc = [line_apply(v[a]) for a in range(N)]
        for c in range(N):
            column = line_apply([v[a][c] for a in range(N)])
            for a in range(N):
                acc[a][c] = acc[a][c] + column[a]
        coeff = coeffs[own]
        out = []
        for a in range(N):
            line = []
            for c in range(N):
                parts = line_parts([sol[node(a, k, c)] for k in range(N)])
                side = min(b, N - 1 - b)
                term = row_even(side, parts)
                if b < 2:
                    term = term + row_odd(side, parts)
                elif b > 2:
                    term = term - row_odd(side, parts)
                value = acc[a][c] + term
                line.append(load[node(a, b, c)] - float(W3[a, b, c]) * coeff * value)
            out.append(line)
        return out

    def gather_plane(f):
        h = []
        for a in range(N):
            h.append([f[a][0] + before(f[a][N - 1])] + f[a][1:N - 1])
        return [[below(h[0][c], h[N - 1][c]) for c in range(N - 1)]] + h[1:N - 1]

    def put_plane(b, values, ref):
        for a in range(N - 1):
            line = list(values[a])
            line.append(after(line[0]))
            for c in range(N):
                ref[node(a, b, c)] = line[c]
                if a == 0:
                    ref[node(N - 1, b, c)] = above(line[c])

    def update_plane(b, scale):
        kind = 0 if 0 < b < N - 1 else (1 if b == 0 else 2)
        values = []
        for a in range(N - 1):
            line = []
            for c in range(N - 1):
                inv = inverse[kind * 4 + (2 if a == 0 else 0) + (1 if c == 0 else 0)] * scale
                line.append(sol[node(a, b, c)] + float(FINE_RELAX / K3[a, b, c]) * inv * total[(b * 4 + a) * 4 + c])
            values.append(line)
        put_plane(b, values, sol)

    def c_copy(cycle, at, theirs, mine):
        return pltpu.make_async_remote_copy(
            src_ref=cgot.at[cycle, own], dst_ref=cgot.at[cycle, theirs],
            send_sem=c_send.at[mine], recv_sem=c_recv.at[cycle, theirs],
            device_id=place(at), device_id_type=MESH)

    def c_wait(cycle, at, theirs, mine):
        pltpu.make_async_remote_copy(
            src_ref=cgot.at[cycle, own], dst_ref=cgot.at[cycle, mine],
            send_sem=c_send.at[mine], recv_sem=c_recv.at[cycle, mine],
            device_id=place(at), device_id_type=MESH).wait()

    def coarse(cycle):
        q = {}
        for b in range(N):
            f = plane_local(b)
            g = [[mix((INTERP[c, k], f[a][c]) for c in range(N)) for k in range(2)] for a in range(N)]
            for i in range(2):
                for k in range(2):
                    h = mix((INTERP[a, i], g[a][k]) for a in range(N))
                    for j in range(2):
                        if INTERP[b, j] != 0:
                            term = scaled(INTERP[b, j], h)
                            q[i, j, k] = q[i, j, k] + term if (i, j, k) in q else term

        def gather(q, j):
            h = [q[i, j, 0] + before(q[i, j, 1]) for i in range(2)]
            return below(h[0], h[1])

        for j in range(2):
            cgot[cycle, own, j] = gather(q, j)
        partners(lambda *p: c_copy(cycle, *p).start())
        partners(lambda *p: c_wait(cycle, *p))
        lines = 2 * REACH
        rc = cgot[cycle, 0:lines, 1] + cgot[cycle, 1:lines + 1, 0]
        inv = cinv[...]
        correction = inv * rc
        coeff = coeffs[1:lines]

        def corners(x):
            right = after(x)
            return {(0, 0): x, (0, 1): right, (1, 0): above(x), (1, 1): above(right)}

        def two(m, x, y):
            return [mix(((m[p, 0], x), (m[p, 1], y))) for p in range(2)]

        for sweep in range(NC - 1):
            nodes = corners(correction)
            v = {(i, j, k): nodes[i, k][j:j + lines - 1] for i in range(2) for j in range(2) for k in range(2)}

            def along(m, v, axis):
                out = {}
                for x in range(2):
                    for y in range(2):
                        key = [(0, x, y), (x, 0, y), (x, y, 0)][axis]
                        key1 = [(1, x, y), (x, 1, y), (x, y, 1)][axis]
                        out[key], out[key1] = two(m, v[key], v[key1])
                return out

            mc = along(COARSE_MASS, v, 2)
            first = along(COARSE_STIFF, along(COARSE_MASS, mc, 1), 0)
            rest = along(COARSE_STIFF, mc, 1)
            third = along(COARSE_MASS, along(COARSE_STIFF, v, 2), 1)
            rest = along(COARSE_MASS, {key: rest[key] + third[key] for key in rest}, 0)
            q2 = {key: coeff * (first[key] + rest[key]) for key in rest}
            low, high = gather(q2, 0), gather(q2, 1)
            zero = jnp.zeros_like(low[0:1])
            image = jnp.concatenate([low, zero], axis=0) + jnp.concatenate([zero, high], axis=0)
            correction = correction + inv * (rc - image)
        ends = [corners(correction[own - 1]), corners(correction[own])]
        for b in range(N):
            mid = {key: mix(((INTERP[b, j], ends[j][key]) for j in range(2))) for key in ends[0]}
            values = []
            for a in range(N - 1):
                pair = [mix(((INTERP[a, i], mid[i, k]) for i in range(2))) for k in range(2)]
                values.append([
                    sol[node(a, b, c)] + mix(((INTERP[c, k], pair[k]) for k in range(2)))
                    for c in range(N - 1)
                ])
            put_plane(b, values, sol)

    def face_copy(slot, side, at):
        return pltpu.make_async_remote_copy(
            src_ref=face.at[side], dst_ref=got.at[slot, 1 - side],
            send_sem=f_send.at[side], recv_sem=f_recv.at[slot, 1 - side],
            device_id=place(at), device_id_type=MESH)

    def face_wait(slot, side, at):
        pltpu.make_async_remote_copy(
            src_ref=face.at[side], dst_ref=got.at[slot, side],
            send_sem=f_send.at[side], recv_sem=f_recv.at[slot, side],
            device_id=place(at), device_id_type=MESH).wait()

    def both(fn):
        @pl.when(row >= 1)
        def _():
            fn(0, row - 1)

        @pl.when(row + 1 < rows)
        def _():
            fn(1, row + 1)

    def step(s, _):
        slot = lax.rem(s, 2)

        @pl.when((lax.rem(s, NPRE + NPOST) == NPRE) & (s < STEPS - 1))
        def _():
            coarse(s // (NPRE + NPOST))

        for side in range(2):
            summed = gather_plane(plane_local(side * (N - 1)))
            for a in range(N - 1):
                for c in range(N - 1):
                    face[side, a * 4 + c] = summed[a][c]
        both(lambda side, at: face_copy(slot, side, at).start())
        for b in range(1, N - 1):
            summed = gather_plane(plane_local(b))
            for a in range(N - 1):
                for c in range(N - 1):
                    total[(b * 4 + a) * 4 + c] = summed[a][c]
        scale = jnp.where(s < STEPS - 1, F32(1.0), F32(0.0))
        for b in range(1, N - 1):
            update_plane(b, scale)
        both(lambda side, at: face_wait(slot, side, at))
        for side in range(2):
            for i in range(16):
                total[side * (N - 1) * 16 + i] = face[side, i] + got[slot, side, i]
            update_plane(side * (N - 1), scale)
        return 0

    lax.fori_loop(0, STEPS, step, 0)

    for b in range(N):
        put_plane(b, [[total[(b * 4 + a) * 4 + c] for c in range(N - 1)] for a in range(N - 1)], load)

    def out(i, _):
        sol_out[i] = sol[i][0:layers]
        res_out[i] = load[i][0:layers]
        return 0

    lax.fori_loop(0, N * N * N, out, 0)


def per_device(sizes, load, kappa, wet):
    layers, _, width = kappa.shape
    nodes = N * N * N
    tile = (2 * layers, width)
    sizes = sizes + (layers, width)
    out = jax.ShapeDtypeStruct((nodes, layers, width), F32)
    vmem = pl.BlockSpec(memory_space=pltpu.VMEM)
    span = 2 * REACH + 1
    dma = pltpu.SemaphoreType.DMA
    solution, residual = pl.pallas_call(
        functools.partial(kernel, sizes),
        out_shape=(out, out),
        in_specs=[vmem] * 3,
        out_specs=(vmem, vmem),
        scratch_shapes=[
            pltpu.VMEM((nodes, layers, width), F32),
            pltpu.VMEM((layers, width), F32),
            pltpu.VMEM((layers, width), F32),
            pltpu.VMEM((nodes,) + tile, F32),
            pltpu.VMEM((span,) + tile, F32),
            pltpu.VMEM((nodes,) + tile, F32),
            pltpu.VMEM((N * 16,) + tile, F32),
            pltpu.VMEM((12,) + tile, F32),
            pltpu.VMEM((2 * REACH,) + tile, F32),
            pltpu.VMEM((2, 16) + tile, F32),
            pltpu.VMEM((2, 2, 16) + tile, F32),
            pltpu.VMEM((CYCLES, span, 2) + tile, F32),
            dma((2,)), dma((2,)), dma((span,)), dma((span,)),
            dma((2,)), dma((2, 2)), dma((span,)), dma((CYCLES, span)),
        ],
        compiler_params=pltpu.CompilerParams(collective_id=0, has_side_effects=True),
    )(load.reshape(nodes, layers, width), kappa.reshape(layers, width), wet.reshape(layers, width))
    return solution.reshape(load.shape), residual.reshape(load.shape)


def solution(mesh):
    sizes = tuple(mesh.shape[name] for name in ("ex", "ey", "lin"))
    field = P(None, None, None, None, ("ey", "lin"), "ex")
    cell = P(None, ("ey", "lin"), "ex")
    return jax.shard_map(
        functools.partial(per_device, sizes), mesh=mesh, in_specs=(field, cell, cell),
        out_specs=(field, field), check_vma=False,
    )
```

```python
import functools
import math

import jax
import jax.numpy as jnp
import numpy as np
from jax import lax
from jax.experimental import pallas as pl
from jax.experimental.pallas import tpu as pltpu
from jax.sharding import PartitionSpec as P

N = 5
CYCLES = 2
NPRE = 2
NPOST = 2
NC = 4
FINE_RELAX = 0.25
COARSE_RELAX = 0.4
REACH = NC + 1
STEPS = CYCLES * (NPRE + NPOST) + 1
HALO = 32
MESH = pl.DeviceIdType.MESH
F32 = jnp.float32


def node_tables():
    points = np.array([-1.0, -math.sqrt(3.0 / 7.0), 0.0, math.sqrt(3.0 / 7.0), 1.0])
    weights = np.array([0.1, 49.0 / 90.0, 32.0 / 45.0, 49.0 / 90.0, 0.1])
    eye_table = np.eye(points.shape[0])
    spread = points[:, None] - points[None, :] + eye_table
    factors = np.prod(spread, axis=1)
    deriv = factors[:, None] / (factors[None, :] * spread)
    deriv = np.where(eye_table > 0, (np.sum(1.0 / spread, axis=1) - 1.0)[:, None], deriv)
    stiff = deriv.T @ (weights[:, None] * deriv)
    mass = eye_table * weights[:, None]
    interp = np.stack([(1.0 - points) / 2.0, (1.0 + points) / 2.0], axis=1)
    return stiff, weights, interp, interp.T @ stiff @ interp, interp.T @ mass @ interp


STIFF, WEIGHTS, INTERP, COARSE_STIFF, COARSE_MASS = node_tables()
D = STIFF / WEIGHTS[:, None]
W3 = WEIGHTS[:, None, None] * WEIGHTS[None, :, None] * WEIGHTS[None, None, :]
DD = np.diag(D)
K3 = W3 * (DD[:, None, None] + DD[None, :, None] + DD[None, None, :])


def node(a, b, c):
    return (a * N + b) * N + c


def line_parts(v):
    twice = v[2] + v[2]
    return (v[0] + v[4]) - twice, (v[1] + v[3]) - twice, v[0] - v[4], v[1] - v[3]


def row_even(i, parts):
    return float((D[i, 0] + D[i, 4]) / 2) * parts[0] + float((D[i, 1] + D[i, 3]) / 2) * parts[1]


def row_odd(i, parts):
    return float((D[i, 0] - D[i, 4]) / 2) * parts[2] + float((D[i, 1] - D[i, 3]) / 2) * parts[3]


def line_apply(v):
    parts = line_parts(v)
    e0, e1, e2 = (row_even(i, parts) for i in range(3))
    o0, o1 = (row_odd(i, parts) for i in range(2))
    return [e0 + o0, e1 + o1, e2, e1 - o1, e0 - o0]


def scaled(factor, value):
    factor = float(factor)
    if factor == 1.0:
        return value
    return factor * value


def mix(pairs):
    total = None
    for factor, value in pairs:
        if abs(float(factor)) < 1e-14:
            continue
        term = scaled(factor, value)
        total = term if total is None else total + term
    return total


def kernel(
    sizes, load_ref, kappa_ref, wet_ref, sol_out, res_out,
    other_load, other_coeff, own_coeff, load, coeffs, sol, total, inverse, cinv, face, got, cgot,
    ex_send, ex_recv, k_send, k_recv, f_send, f_recv, c_send, c_recv,
):
    ex_count, ey_count, lin_count, layers, width = sizes
    ex, ey, lin = lax.axis_index("ex"), lax.axis_index("ey"), lax.axis_index("lin")
    rows = ey_count * lin_count
    row = ey * lin_count + lin
    own = REACH

    sub = lax.broadcasted_iota(jnp.int32, (2 * layers, width), 0)
    lane = lax.broadcasted_iota(jnp.int32, (2 * layers, width), 1)
    layer = sub % layers
    bottom, top = layer == 0, layer == layers - 1
    first_lane, last_lane = lane == 0, lane == width - 1
    near = jnp.where(ex == 0, lane, width - 1 - lane)
    real = (sub < layers) | (near < HALO)

    def like(mask, x):
        return jnp.broadcast_to(mask, x.shape) if x.ndim == 3 else mask

    def before(x):
        y = pltpu.roll(x, 1, x.ndim - 1)
        return jnp.where(like(first_lane, x), pltpu.roll(y, layers, x.ndim - 2), y)

    def after(x):
        y = pltpu.roll(x, width - 1, x.ndim - 1)
        return jnp.where(like(last_lane, x), pltpu.roll(y, layers, x.ndim - 2), y)

    def below(low, high):
        return jnp.where(like(bottom, low), low, low + pltpu.roll(high, 1, low.ndim - 2))

    def above(low):
        return jnp.where(like(top, low), 0.0, pltpu.roll(low, 2 * layers - 1, low.ndim - 2))

    def place(at):
        return (ex, at // lin_count, at % lin_count)

    def partners(fn):
        for d in range(1, REACH + 1):
            @pl.when(row >= d)
            def _():
                fn(row - d, own + d, own - d)

            @pl.when(row + d < rows)
            def _():
                fn(row + d, own - d, own + d)

    coeffs[...] = jnp.zeros_like(coeffs)
    cgot[...] = jnp.zeros_like(cgot)
    got[...] = jnp.zeros_like(got)
    barrier = pltpu.get_barrier_semaphore()
    pl.semaphore_signal(barrier, inc=1, device_id=(1 - ex, ey, lin), device_id_type=MESH)
    partners(lambda at, theirs, mine: pl.semaphore_signal(
        barrier, inc=1, device_id=place(at), device_id_type=MESH))

    coeff_own = kappa_ref[...] * jnp.where(wet_ref[...] == 1, F32(1.0), F32(0.05))
    own_coeff[...] = coeff_own

    pl.semaphore_wait(barrier, 1 + jnp.minimum(row, REACH) + jnp.minimum(rows - 1 - row, REACH))

    def ex_copy(src, dst, i):
        return pltpu.make_async_remote_copy(
            src_ref=src, dst_ref=dst, send_sem=ex_send.at[i], recv_sem=ex_recv.at[i],
            device_id=(1 - ex, ey, lin), device_id_type=MESH)

    coeff_copy = ex_copy(own_coeff, other_coeff, 0)
    load_copy = ex_copy(load_ref, other_load, 1)
    coeff_copy.start()
    load_copy.start()
    sol[...] = jnp.zeros_like(sol)
    coeff_copy.wait()
    coeffs[own] = jnp.where(real, jnp.concatenate([coeff_own, other_coeff[...]], axis=0), 0.0)

    def k_copy(at, theirs, mine):
        return pltpu.make_async_remote_copy(
            src_ref=coeffs.at[own], dst_ref=coeffs.at[theirs],
            send_sem=k_send.at[mine], recv_sem=k_recv.at[theirs],
            device_id=place(at), device_id_type=MESH)

    def k_wait(at, theirs, mine):
        pltpu.make_async_remote_copy(
            src_ref=coeffs.at[own], dst_ref=coeffs.at[mine],
            send_sem=k_send.at[mine], recv_sem=k_recv.at[mine],
            device_id=place(at), device_id_type=MESH).wait()

    partners(lambda *p: k_copy(*p).start())
    load_copy.wait()

    def join(i, _):
        load[i] = jnp.where(real, jnp.concatenate([load_ref[i], other_load[i]], axis=0), 0.0)
        return 0

    lax.fori_loop(0, N * N * N, join, 0)
    def inverted(x):
        return jnp.where(x > 0.0, 1.0 / jnp.where(x > 0.0, x, 1.0), 0.0)

    def invert():
        partners(k_wait)
        here = coeffs[own]
        for kind, x in enumerate((here, here + coeffs[own - 1], here + coeffs[own + 1])):
            xc = x + before(x)
            for slot, y in enumerate((x, xc, below(x, x), below(xc, xc))):
                inverse[kind * 4 + slot] = inverted(y)
        pairs = coeffs[0:2 * REACH] + coeffs[1:2 * REACH + 1]
        pairs = pairs + before(pairs)
        pairs = below(pairs, pairs)
        corner = 3.0 * COARSE_STIFF[0, 0] * COARSE_MASS[0, 0] ** 2
        cinv[...] = float(COARSE_RELAX / corner) * inverted(pairs)

    def plane_local(b):
        v = [[sol[node(a, b, c)] for c in range(N)] for a in range(N)]
        acc = [line_apply(v[a]) for a in range(N)]
        for c in range(N):
            column = line_apply([v[a][c] for a in range(N)])
            for a in range(N):
                acc[a][c] = acc[a][c] + column[a]
        coeff = coeffs[own]
        out = []
        for a in range(N):
            line = []
            for c in range(N):
                parts = line_parts([sol[node(a, k, c)] for k in range(N)])
                side = min(b, N - 1 - b)
                term = row_even(side, parts)
                if b < 2:
                    term = term + row_odd(side, parts)
                elif b > 2:
                    term = term - row_odd(side, parts)
                value = acc[a][c] + term
                line.append(load[node(a, b, c)] - float(W3[a, b, c]) * coeff * value)
            out.append(line)
        return out

    def gather_plane(f):
        h = []
        for a in range(N):
            h.append([f[a][0] + before(f[a][N - 1])] + f[a][1:N - 1])
        return [[below(h[0][c], h[N - 1][c]) for c in range(N - 1)]] + h[1:N - 1]

    def put_plane(b, values, ref):
        for a in range(N - 1):
            line = list(values[a])
            line.append(after(line[0]))
            for c in range(N):
                ref[node(a, b, c)] = line[c]
                if a == 0:
                    ref[node(N - 1, b, c)] = above(line[c])

    def update_plane(b, scale):
        kind = 0 if 0 < b < N - 1 else (1 if b == 0 else 2)
        values = []
        for a in range(N - 1):
            line = []
            for c in range(N - 1):
                inv = inverse[kind * 4 + (2 if a == 0 else 0) + (1 if c == 0 else 0)] * scale
                line.append(sol[node(a, b, c)] + float(FINE_RELAX / K3[a, b, c]) * inv * total[(b * 4 + a) * 4 + c])
            values.append(line)
        put_plane(b, values, sol)

    def c_copy(cycle, at, theirs, mine):
        return pltpu.make_async_remote_copy(
            src_ref=cgot.at[cycle, own], dst_ref=cgot.at[cycle, theirs],
            send_sem=c_send.at[mine], recv_sem=c_recv.at[cycle, theirs],
            device_id=place(at), device_id_type=MESH)

    def c_wait(cycle, at, theirs, mine):
        pltpu.make_async_remote_copy(
            src_ref=cgot.at[cycle, own], dst_ref=cgot.at[cycle, mine],
            send_sem=c_send.at[mine], recv_sem=c_recv.at[cycle, mine],
            device_id=place(at), device_id_type=MESH).wait()

    def gather(q, j):
        h = [q[i, j, 0] + before(q[i, j, 1]) for i in range(2)]
        return below(h[0], h[1])

    def coarse_send(cycle):
        q = {}
        for b in range(N):
            side = {0: 0, N - 1: 1}.get(b)
            f = [[total[(b * 4 + a) * 4 + c] if side is None else face[side, a * 4 + c]
                  for c in range(N - 1)] for a in range(N - 1)]
            g = [[mix((INTERP[c, k], f[a][c]) for c in range(N - 1)) for k in range(2)] for a in range(N - 1)]
            for i in range(2):
                for k in range(2):
                    h = mix((INTERP[a, i], g[a][k]) for a in range(N - 1))
                    for j in range(2):
                        if INTERP[b, j] != 0:
                            term = scaled(INTERP[b, j], h)
                            q[i, j, k] = q[i, j, k] + term if (i, j, k) in q else term
        for j in range(2):
            cgot[cycle, own, j] = gather(q, j)
        partners(lambda *p: c_copy(cycle, *p).start())

    def correct(cycle):
        partners(lambda *p: c_wait(cycle, *p))
        lines = 2 * REACH
        rc = cgot[cycle, 0:lines, 1] + cgot[cycle, 1:lines + 1, 0]
        inv = cinv[...]
        correction = inv * rc
        coeff = coeffs[1:lines]

        def corners(x):
            right = after(x)
            return {(0, 0): x, (0, 1): right, (1, 0): above(x), (1, 1): above(right)}

        def two(m, x, y):
            return [mix(((m[p, 0], x), (m[p, 1], y))) for p in range(2)]

        for sweep in range(NC - 1):
            nodes = corners(correction)
            v = {(i, j, k): nodes[i, k][j:j + lines - 1] for i in range(2) for j in range(2) for k in range(2)}

            def along(m, v, axis):
                out = {}
                for x in range(2):
                    for y in range(2):
                        key = [(0, x, y), (x, 0, y), (x, y, 0)][axis]
                        key1 = [(1, x, y), (x, 1, y), (x, y, 1)][axis]
                        out[key], out[key1] = two(m, v[key], v[key1])
                return out

            mc = along(COARSE_MASS, v, 2)
            first = along(COARSE_STIFF, along(COARSE_MASS, mc, 1), 0)
            rest = along(COARSE_STIFF, mc, 1)
            third = along(COARSE_MASS, along(COARSE_STIFF, v, 2), 1)
            rest = along(COARSE_MASS, {key: rest[key] + third[key] for key in rest}, 0)
            q2 = {key: coeff * (first[key] + rest[key]) for key in rest}
            low, high = gather(q2, 0), gather(q2, 1)
            zero = jnp.zeros_like(low[0:1])
            image = jnp.concatenate([low, zero], axis=0) + jnp.concatenate([zero, high], axis=0)
            correction = correction + inv * (rc - image)
        ends = [corners(correction[own - 2 + m]) for m in range(4)]

        def interpolated(k, b):
            return {key: mix(((INTERP[b, j], ends[k + j][key]) for j in range(2))) for key in ends[0]}

        def operated(k, b):
            coeff = coeffs[own - 1 + k]
            half = {key: (0.5 * coeff) * value for key, value in interpolated(k, b).items()}
            f = [[None] * N for _ in range(N)]

            def put(a, c, value):
                f[a][c] = value if f[a][c] is None else f[a][c] + value

            rise_c = [half[i, 1] - half[i, 0] for i in range(2)]
            rise_a = [half[1, i] - half[0, i] for i in range(2)]
            for n in range(N):
                value = float(WEIGHTS[n] * WEIGHTS[b]) * mix(((INTERP[n, i], rise_c[i]) for i in range(2)))
                put(n, 0, value)
                put(n, N - 1, -value)
                value = float(WEIGHTS[n] * WEIGHTS[b]) * mix(((INTERP[n, i], rise_a[i]) for i in range(2)))
                put(0, n, value)
                put(N - 1, n, -value)
            if b in (0, N - 1):
                sign = 0.5 if b == 0 else -0.5
                rise_b = {key: (sign * coeff) * (ends[k + 1][key] - ends[k][key]) for key in ends[0]}
                for a in range(N):
                    pair = [mix(((INTERP[a, i], rise_b[i, x]) for i in range(2))) for x in range(2)]
                    for c in range(N):
                        put(a, c, float(WEIGHTS[a] * WEIGHTS[c]) * mix(((INTERP[c, x], pair[x]) for x in range(2))))
            return f

        for b in range(N):
            sums = [gather_plane(operated(1, b))]
            if b == 0:
                sums.append(gather_plane(operated(0, N - 1)))
            if b == N - 1:
                sums.append(gather_plane(operated(2, 0)))
            mid = interpolated(1, b)
            for a in range(N - 1):
                pair = [mix(((INTERP[a, i], mid[i, k]) for i in range(2))) for k in range(2)]
                for c in range(N - 1):
                    at = node(a, b, c)
                    sol[at] = sol[at] + mix(((INTERP[c, k], pair[k]) for k in range(2)))
                    if sums[0][a][c] is not None:
                        at = (b * 4 + a) * 4 + c
                        value = total[at]
                        for one in sums:
                            value = value + one[a][c]
                        total[at] = value

    def face_copy(slot, side, at):
        return pltpu.make_async_remote_copy(
            src_ref=face.at[side], dst_ref=got.at[slot, 1 - side],
            send_sem=f_send.at[side], recv_sem=f_recv.at[slot, 1 - side],
            device_id=place(at), device_id_type=MESH)

    def face_wait(slot, side, at):
        pltpu.make_async_remote_copy(
            src_ref=face.at[side], dst_ref=got.at[slot, side],
            send_sem=f_send.at[side], recv_sem=f_recv.at[slot, side],
            device_id=place(at), device_id_type=MESH).wait()

    def both(fn):
        @pl.when(row >= 1)
        def _():
            fn(0, row - 1)

        @pl.when(row + 1 < rows)
        def _():
            fn(1, row + 1)

    def step(s, _):
        slot = lax.rem(s, 2)

        cycle = s // (NPRE + NPOST)
        coarse = (lax.rem(s, NPRE + NPOST) == NPRE) & (s < STEPS - 1)

        for side in range(2):
            summed = gather_plane(plane_local(side * (N - 1)))
            for a in range(N - 1):
                for c in range(N - 1):
                    face[side, a * 4 + c] = summed[a][c]
        both(lambda side, at: face_copy(slot, side, at).start())
        for b in range(1, N - 1):
            summed = gather_plane(plane_local(b))
            for a in range(N - 1):
                for c in range(N - 1):
                    total[(b * 4 + a) * 4 + c] = summed[a][c]
        scale = jnp.where(s < STEPS - 1, F32(1.0), F32(0.0))

        @pl.when(s == 0)
        def _():
            invert()

        @pl.when(coarse)
        def _():
            coarse_send(cycle)

        @pl.when(jnp.logical_not(coarse))
        def _():
            for b in range(1, N - 1):
                update_plane(b, scale)

        both(lambda side, at: face_wait(slot, side, at))
        for side in range(2):
            for i in range(16):
                total[side * (N - 1) * 16 + i] = face[side, i] + got[slot, side, i]

        @pl.when(coarse)
        def _():
            correct(cycle)
            for b in range(1, N - 1):
                update_plane(b, scale)

        for side in range(2):
            update_plane(side * (N - 1), scale)
        return 0

    lax.fori_loop(0, STEPS, step, 0)

    for b in range(N):
        put_plane(b, [[total[(b * 4 + a) * 4 + c] for c in range(N - 1)] for a in range(N - 1)], load)

    def out(i, _):
        sol_out[i] = sol[i][0:layers]
        res_out[i] = load[i][0:layers]
        return 0

    lax.fori_loop(0, N * N * N, out, 0)


def per_device(sizes, load, kappa, wet):
    layers, _, width = kappa.shape
    nodes = N * N * N
    tile = (2 * layers, width)
    sizes = sizes + (layers, width)
    out = jax.ShapeDtypeStruct((nodes, layers, width), F32)
    vmem = pl.BlockSpec(memory_space=pltpu.VMEM)
    span = 2 * REACH + 1
    dma = pltpu.SemaphoreType.DMA
    solution, residual = pl.pallas_call(
        functools.partial(kernel, sizes),
        out_shape=(out, out),
        in_specs=[vmem] * 3,
        out_specs=(vmem, vmem),
        scratch_shapes=[
            pltpu.VMEM((nodes, layers, width), F32),
            pltpu.VMEM((layers, width), F32),
            pltpu.VMEM((layers, width), F32),
            pltpu.VMEM((nodes,) + tile, F32),
            pltpu.VMEM((span,) + tile, F32),
            pltpu.VMEM((nodes,) + tile, F32),
            pltpu.VMEM((N * 16,) + tile, F32),
            pltpu.VMEM((12,) + tile, F32),
            pltpu.VMEM((2 * REACH,) + tile, F32),
            pltpu.VMEM((2, 16) + tile, F32),
            pltpu.VMEM((2, 2, 16) + tile, F32),
            pltpu.VMEM((CYCLES, span, 2) + tile, F32),
            dma((2,)), dma((2,)), dma((span,)), dma((span,)),
            dma((2,)), dma((2, 2)), dma((span,)), dma((CYCLES, span)),
        ],
        compiler_params=pltpu.CompilerParams(collective_id=0, has_side_effects=True),
    )(load.reshape(nodes, layers, width), kappa.reshape(layers, width), wet.reshape(layers, width))
    return solution.reshape(load.shape), residual.reshape(load.shape)


def solution(mesh):
    sizes = tuple(mesh.shape[name] for name in ("ex", "ey", "lin"))
    field = P(None, None, None, None, ("ey", "lin"), "ex")
    cell = P(None, ("ey", "lin"), "ex")
    return jax.shard_map(
        functools.partial(per_device, sizes), mesh=mesh, in_specs=(field, cell, cell),
        out_specs=(field, field), check_vma=False,
    )
```

```python
import functools
import math

import jax
import jax.numpy as jnp
import numpy as np
from jax import lax
from jax.experimental import pallas as pl
from jax.experimental.pallas import tpu as pltpu
from jax.sharding import PartitionSpec as P

N = 5
CYCLES = 2
NPRE = 2
NPOST = 2
NC = 4
FINE_RELAX = 0.25
COARSE_RELAX = 0.4
REACH = NC + 1
STEPS = CYCLES * (NPRE + NPOST) + 1
HALO = 32
MESH = pl.DeviceIdType.MESH
F32 = jnp.float32


def node_tables():
    points = np.array([-1.0, -math.sqrt(3.0 / 7.0), 0.0, math.sqrt(3.0 / 7.0), 1.0])
    weights = np.array([0.1, 49.0 / 90.0, 32.0 / 45.0, 49.0 / 90.0, 0.1])
    eye_table = np.eye(points.shape[0])
    spread = points[:, None] - points[None, :] + eye_table
    factors = np.prod(spread, axis=1)
    deriv = factors[:, None] / (factors[None, :] * spread)
    deriv = np.where(eye_table > 0, (np.sum(1.0 / spread, axis=1) - 1.0)[:, None], deriv)
    stiff = deriv.T @ (weights[:, None] * deriv)
    mass = eye_table * weights[:, None]
    interp = np.stack([(1.0 - points) / 2.0, (1.0 + points) / 2.0], axis=1)
    return stiff, weights, interp, interp.T @ stiff @ interp, interp.T @ mass @ interp


STIFF, WEIGHTS, INTERP, COARSE_STIFF, COARSE_MASS = node_tables()
D = STIFF / WEIGHTS[:, None]
W3 = WEIGHTS[:, None, None] * WEIGHTS[None, :, None] * WEIGHTS[None, None, :]
DD = np.diag(D)
K3 = W3 * (DD[:, None, None] + DD[None, :, None] + DD[None, None, :])


def node(a, b, c):
    return (a * N + b) * N + c


def line_parts(v):
    twice = v[2] + v[2]
    return (v[0] + v[4]) - twice, (v[1] + v[3]) - twice, v[0] - v[4], v[1] - v[3]


def row_even(i, parts):
    return float((D[i, 0] + D[i, 4]) / 2) * parts[0] + float((D[i, 1] + D[i, 3]) / 2) * parts[1]


def row_odd(i, parts):
    return float((D[i, 0] - D[i, 4]) / 2) * parts[2] + float((D[i, 1] - D[i, 3]) / 2) * parts[3]


def line_apply(v):
    parts = line_parts(v)
    e0, e1, e2 = (row_even(i, parts) for i in range(3))
    o0, o1 = (row_odd(i, parts) for i in range(2))
    return [e0 + o0, e1 + o1, e2, e1 - o1, e0 - o0]


def scaled(factor, value):
    factor = float(factor)
    if factor == 1.0:
        return value
    return factor * value


def mix(pairs):
    total = None
    for factor, value in pairs:
        if abs(float(factor)) < 1e-14:
            continue
        term = scaled(factor, value)
        total = term if total is None else total + term
    return total


def kernel(
    sizes, load_ref, kappa_ref, wet_ref, sol_out, res_out,
    other_load, other_coeff, own_coeff, load, coeffs, sol, total, inverse, cinv, face, packed, got, cgot,
    ex_send, ex_recv, k_send, k_recv, f_send, f_recv, c_send, c_recv,
):
    ex_count, ey_count, lin_count, layers, width = sizes
    ex, ey, lin = lax.axis_index("ex"), lax.axis_index("ey"), lax.axis_index("lin")
    rows = ey_count * lin_count
    row = ey * lin_count + lin
    own = REACH

    sub = lax.broadcasted_iota(jnp.int32, (2 * layers, width), 0)
    lane = lax.broadcasted_iota(jnp.int32, (2 * layers, width), 1)
    layer = sub % layers
    bottom, top = layer == 0, layer == layers - 1
    first_lane, last_lane = lane == 0, lane == width - 1
    near = jnp.where(ex == 0, lane, width - 1 - lane)
    real = (sub < layers) | (near < HALO)

    def like(mask, x):
        return jnp.broadcast_to(mask, x.shape) if x.ndim == 3 else mask

    def before(x):
        y = pltpu.roll(x, 1, x.ndim - 1)
        return jnp.where(like(first_lane, x), pltpu.roll(y, layers, x.ndim - 2), y)

    def after(x):
        y = pltpu.roll(x, width - 1, x.ndim - 1)
        return jnp.where(like(last_lane, x), pltpu.roll(y, layers, x.ndim - 2), y)

    def below(low, high):
        return jnp.where(like(bottom, low), low, low + pltpu.roll(high, 1, low.ndim - 2))

    def above(low):
        return jnp.where(like(top, low), 0.0, pltpu.roll(low, 2 * layers - 1, low.ndim - 2))

    def place(at):
        return (ex, at // lin_count, at % lin_count)

    def partners(fn):
        for d in range(1, REACH + 1):
            @pl.when(row >= d)
            def _():
                fn(row - d, own + d, own - d)

            @pl.when(row + d < rows)
            def _():
                fn(row + d, own - d, own + d)

    coeffs[...] = jnp.zeros_like(coeffs)
    cgot[...] = jnp.zeros_like(cgot)
    got[...] = jnp.zeros_like(got)
    barrier = pltpu.get_barrier_semaphore()
    pl.semaphore_signal(barrier, inc=1, device_id=(1 - ex, ey, lin), device_id_type=MESH)
    partners(lambda at, theirs, mine: pl.semaphore_signal(
        barrier, inc=1, device_id=place(at), device_id_type=MESH))

    coeff_own = kappa_ref[...] * jnp.where(wet_ref[...] == 1, F32(1.0), F32(0.05))
    own_coeff[...] = coeff_own

    pl.semaphore_wait(barrier, 1 + jnp.minimum(row, REACH) + jnp.minimum(rows - 1 - row, REACH))

    def ex_copy(src, dst, i):
        return pltpu.make_async_remote_copy(
            src_ref=src, dst_ref=dst, send_sem=ex_send.at[i], recv_sem=ex_recv.at[i],
            device_id=(1 - ex, ey, lin), device_id_type=MESH)

    coeff_copy = ex_copy(own_coeff, other_coeff, 0)
    load_copy = ex_copy(load_ref, other_load, 1)
    coeff_copy.start()
    load_copy.start()
    sol[...] = jnp.zeros_like(sol)
    coeff_copy.wait()
    coeffs[own] = jnp.where(real, jnp.concatenate([coeff_own, other_coeff[...]], axis=0), 0.0)

    def k_copy(at, theirs, mine):
        return pltpu.make_async_remote_copy(
            src_ref=coeffs.at[own], dst_ref=coeffs.at[theirs],
            send_sem=k_send.at[mine], recv_sem=k_recv.at[theirs],
            device_id=place(at), device_id_type=MESH)

    def k_wait(at, theirs, mine):
        pltpu.make_async_remote_copy(
            src_ref=coeffs.at[own], dst_ref=coeffs.at[mine],
            send_sem=k_send.at[mine], recv_sem=k_recv.at[mine],
            device_id=place(at), device_id_type=MESH).wait()

    partners(lambda *p: k_copy(*p).start())
    load_copy.wait()

    def join(i, _):
        load[i] = jnp.where(real, jnp.concatenate([load_ref[i], other_load[i]], axis=0), 0.0)
        return 0

    lax.fori_loop(0, N * N * N, join, 0)
    def inverted(x):
        return jnp.where(x > 0.0, 1.0 / jnp.where(x > 0.0, x, 1.0), 0.0)

    def invert():
        partners(k_wait)
        here = coeffs[own]
        for kind, x in enumerate((here, here + coeffs[own - 1], here + coeffs[own + 1])):
            xc = x + before(x)
            for slot, y in enumerate((x, xc, below(x, x), below(xc, xc))):
                inverse[kind * 4 + slot] = inverted(y)
        pairs = coeffs[0:2 * REACH] + coeffs[1:2 * REACH + 1]
        pairs = pairs + before(pairs)
        pairs = below(pairs, pairs)
        corner = 3.0 * COARSE_STIFF[0, 0] * COARSE_MASS[0, 0] ** 2
        cinv[...] = float(COARSE_RELAX / corner) * inverted(pairs)

    def plane_local(b):
        v = [[sol[node(a, b, c)] for c in range(N)] for a in range(N)]
        acc = [line_apply(v[a]) for a in range(N)]
        for c in range(N):
            column = line_apply([v[a][c] for a in range(N)])
            for a in range(N):
                acc[a][c] = acc[a][c] + column[a]
        coeff = coeffs[own]
        out = []
        for a in range(N):
            line = []
            for c in range(N):
                parts = line_parts([sol[node(a, k, c)] for k in range(N)])
                side = min(b, N - 1 - b)
                term = row_even(side, parts)
                if b < 2:
                    term = term + row_odd(side, parts)
                elif b > 2:
                    term = term - row_odd(side, parts)
                value = acc[a][c] + term
                line.append(load[node(a, b, c)] - float(W3[a, b, c]) * coeff * value)
            out.append(line)
        return out

    def gather_plane(f):
        h = []
        for a in range(N):
            h.append([f[a][0] + before(f[a][N - 1])] + f[a][1:N - 1])
        return [[below(h[0][c], h[N - 1][c]) for c in range(N - 1)]] + h[1:N - 1]

    def put_plane(b, values, ref):
        for a in range(N - 1):
            line = list(values[a])
            line.append(after(line[0]))
            for c in range(N):
                ref[node(a, b, c)] = line[c]
                if a == 0:
                    ref[node(N - 1, b, c)] = above(line[c])

    def update_plane(b, scale):
        kind = 0 if 0 < b < N - 1 else (1 if b == 0 else 2)
        values = []
        for a in range(N - 1):
            line = []
            for c in range(N - 1):
                inv = inverse[kind * 4 + (2 if a == 0 else 0) + (1 if c == 0 else 0)] * scale
                line.append(sol[node(a, b, c)] + float(FINE_RELAX / K3[a, b, c]) * inv * total[(b * 4 + a) * 4 + c])
            values.append(line)
        put_plane(b, values, sol)

    def c_copy(cycle, at, theirs, mine):
        return pltpu.make_async_remote_copy(
            src_ref=cgot.at[cycle, own], dst_ref=cgot.at[cycle, theirs],
            send_sem=c_send.at[mine], recv_sem=c_recv.at[cycle, theirs],
            device_id=place(at), device_id_type=MESH)

    def c_wait(cycle, at, theirs, mine):
        pltpu.make_async_remote_copy(
            src_ref=cgot.at[cycle, own], dst_ref=cgot.at[cycle, mine],
            send_sem=c_send.at[mine], recv_sem=c_recv.at[cycle, mine],
            device_id=place(at), device_id_type=MESH).wait()

    def gather(q, j):
        h = [q[i, j, 0] + before(q[i, j, 1]) for i in range(2)]
        return below(h[0], h[1])

    def coarse_send(cycle):
        q = {}
        for b in range(N):
            side = {0: 0, N - 1: 1}.get(b)
            f = [[total[(b * 4 + a) * 4 + c] if side is None else face[side, a * 4 + c]
                  for c in range(N - 1)] for a in range(N - 1)]
            g = [[mix((INTERP[c, k], f[a][c]) for c in range(N - 1)) for k in range(2)] for a in range(N - 1)]
            for i in range(2):
                for k in range(2):
                    h = mix((INTERP[a, i], g[a][k]) for a in range(N - 1))
                    for j in range(2):
                        if INTERP[b, j] != 0:
                            term = scaled(INTERP[b, j], h)
                            q[i, j, k] = q[i, j, k] + term if (i, j, k) in q else term
        for j in range(2):
            cgot[cycle, own, j] = gather(q, j)
        partners(lambda *p: c_copy(cycle, *p).start())

    def correct(cycle):
        partners(lambda *p: c_wait(cycle, *p))
        lines = 2 * REACH
        rc = cgot[cycle, 0:lines, 1] + cgot[cycle, 1:lines + 1, 0]
        inv = cinv[...]
        correction = inv * rc
        coeff = coeffs[1:lines]

        def corners(x):
            right = after(x)
            return {(0, 0): x, (0, 1): right, (1, 0): above(x), (1, 1): above(right)}

        def two(m, x, y):
            return [mix(((m[p, 0], x), (m[p, 1], y))) for p in range(2)]

        for sweep in range(NC - 1):
            nodes = corners(correction)
            v = {(i, j, k): nodes[i, k][j:j + lines - 1] for i in range(2) for j in range(2) for k in range(2)}

            def along(m, v, axis):
                out = {}
                for x in range(2):
                    for y in range(2):
                        key = [(0, x, y), (x, 0, y), (x, y, 0)][axis]
                        key1 = [(1, x, y), (x, 1, y), (x, y, 1)][axis]
                        out[key], out[key1] = two(m, v[key], v[key1])
                return out

            mc = along(COARSE_MASS, v, 2)
            first = along(COARSE_STIFF, along(COARSE_MASS, mc, 1), 0)
            rest = along(COARSE_STIFF, mc, 1)
            third = along(COARSE_MASS, along(COARSE_STIFF, v, 2), 1)
            rest = along(COARSE_MASS, {key: rest[key] + third[key] for key in rest}, 0)
            q2 = {key: coeff * (first[key] + rest[key]) for key in rest}
            low, high = gather(q2, 0), gather(q2, 1)
            zero = jnp.zeros_like(low[0:1])
            image = jnp.concatenate([low, zero], axis=0) + jnp.concatenate([zero, high], axis=0)
            correction = correction + inv * (rc - image)
        ends = [corners(correction[own - 2 + m]) for m in range(4)]

        def interpolated(k, b):
            return {key: mix(((INTERP[b, j], ends[k + j][key]) for j in range(2))) for key in ends[0]}

        def operated(k, b):
            coeff = coeffs[own - 1 + k]
            half = {key: (0.5 * coeff) * value for key, value in interpolated(k, b).items()}
            f = [[None] * N for _ in range(N)]

            def put(a, c, value):
                f[a][c] = value if f[a][c] is None else f[a][c] + value

            rise_c = [half[i, 1] - half[i, 0] for i in range(2)]
            rise_a = [half[1, i] - half[0, i] for i in range(2)]
            for n in range(N):
                value = float(WEIGHTS[n] * WEIGHTS[b]) * mix(((INTERP[n, i], rise_c[i]) for i in range(2)))
                put(n, 0, value)
                put(n, N - 1, -value)
                value = float(WEIGHTS[n] * WEIGHTS[b]) * mix(((INTERP[n, i], rise_a[i]) for i in range(2)))
                put(0, n, value)
                put(N - 1, n, -value)
            if b in (0, N - 1):
                sign = 0.5 if b == 0 else -0.5
                rise_b = {key: (sign * coeff) * (ends[k + 1][key] - ends[k][key]) for key in ends[0]}
                for a in range(N):
                    pair = [mix(((INTERP[a, i], rise_b[i, x]) for i in range(2))) for x in range(2)]
                    for c in range(N):
                        put(a, c, float(WEIGHTS[a] * WEIGHTS[c]) * mix(((INTERP[c, x], pair[x]) for x in range(2))))
            return f

        for b in range(N):
            sums = [gather_plane(operated(1, b))]
            if b == 0:
                sums.append(gather_plane(operated(0, N - 1)))
            if b == N - 1:
                sums.append(gather_plane(operated(2, 0)))
            mid = interpolated(1, b)
            for a in range(N - 1):
                pair = [mix(((INTERP[a, i], mid[i, k]) for i in range(2))) for k in range(2)]
                for c in range(N - 1):
                    at = node(a, b, c)
                    sol[at] = sol[at] + mix(((INTERP[c, k], pair[k]) for k in range(2)))
                    if sums[0][a][c] is not None:
                        at = (b * 4 + a) * 4 + c
                        value = total[at]
                        for one in sums:
                            value = value + one[a][c]
                        total[at] = value

    fold = width // HALO
    block = lax.rem(lane + jnp.where(ex == 0, 0, HALO - 1), width) // HALO
    lower = sub < layers

    def swap(x):
        return pltpu.roll(x, layers, 0)

    def pack(side, x):
        for p in range(8):
            packed[side, p] = jnp.where(lower, x[2 * p], swap(x[2 * p + 1]))
        for p in range(8 // fold):
            halves = []
            for h in range(2):
                group = x[(2 * p + h) * fold:(2 * p + h + 1) * fold]
                mixed = group[0]
                for j in range(1, fold):
                    mixed = jnp.where(block == j, pltpu.roll(group[j], HALO * j, 1), mixed)
                halves.append(mixed)
            packed[side, 8 + p] = jnp.where(lower, swap(halves[0]), halves[1])

    def unpack(slot, side):
        x = []
        for p in range(8 // fold):
            tile = got[slot, side, 8 + p]
            for half in (swap(tile), tile):
                for j in range(fold):
                    other = half if j == 0 else pltpu.roll(half, width - HALO * j, 1)
                    n = len(x)
                    mine = got[slot, side, n // 2]
                    mine = mine if n % 2 == 0 else swap(mine)
                    x.append(jnp.where(lower, mine, jnp.where(block == 0, other, 0.0)))
        return x

    def face_copy(slot, side, at):
        return pltpu.make_async_remote_copy(
            src_ref=packed.at[side], dst_ref=got.at[slot, 1 - side],
            send_sem=f_send.at[side], recv_sem=f_recv.at[slot, 1 - side],
            device_id=place(at), device_id_type=MESH)

    def face_wait(slot, side, at):
        pltpu.make_async_remote_copy(
            src_ref=packed.at[side], dst_ref=got.at[slot, side],
            send_sem=f_send.at[side], recv_sem=f_recv.at[slot, side],
            device_id=place(at), device_id_type=MESH).wait()

    def both(fn):
        @pl.when(row >= 1)
        def _():
            fn(0, row - 1)

        @pl.when(row + 1 < rows)
        def _():
            fn(1, row + 1)

    def step(s, _):
        slot = lax.rem(s, 2)

        cycle = s // (NPRE + NPOST)
        coarse = (lax.rem(s, NPRE + NPOST) == NPRE) & (s < STEPS - 1)

        for side in range(2):
            summed = gather_plane(plane_local(side * (N - 1)))
            for a in range(N - 1):
                for c in range(N - 1):
                    face[side, a * 4 + c] = summed[a][c]
            pack(side, [value for values in summed for value in values])
        both(lambda side, at: face_copy(slot, side, at).start())
        for b in range(1, N - 1):
            summed = gather_plane(plane_local(b))
            for a in range(N - 1):
                for c in range(N - 1):
                    total[(b * 4 + a) * 4 + c] = summed[a][c]
        scale = jnp.where(s < STEPS - 1, F32(1.0), F32(0.0))

        @pl.when(s == 0)
        def _():
            invert()

        @pl.when(coarse)
        def _():
            coarse_send(cycle)

        @pl.when(jnp.logical_not(coarse))
        def _():
            for b in range(1, N - 1):
                update_plane(b, scale)

        both(lambda side, at: face_wait(slot, side, at))
        for side in range(2):
            theirs = unpack(slot, side)
            for i in range(16):
                total[side * (N - 1) * 16 + i] = face[side, i] + theirs[i]

        @pl.when(coarse)
        def _():
            correct(cycle)
            for b in range(1, N - 1):
                update_plane(b, scale)

        for side in range(2):
            update_plane(side * (N - 1), scale)
        return 0

    lax.fori_loop(0, STEPS, step, 0)

    for b in range(N):
        put_plane(b, [[total[(b * 4 + a) * 4 + c] for c in range(N - 1)] for a in range(N - 1)], load)

    def out(i, _):
        sol_out[i] = sol[i][0:layers]
        res_out[i] = load[i][0:layers]
        return 0

    lax.fori_loop(0, N * N * N, out, 0)


def per_device(sizes, load, kappa, wet):
    layers, _, width = kappa.shape
    nodes = N * N * N
    tile = (2 * layers, width)
    sizes = sizes + (layers, width)
    out = jax.ShapeDtypeStruct((nodes, layers, width), F32)
    vmem = pl.BlockSpec(memory_space=pltpu.VMEM)
    span = 2 * REACH + 1
    messages = 8 + 8 * HALO // width
    dma = pltpu.SemaphoreType.DMA
    solution, residual = pl.pallas_call(
        functools.partial(kernel, sizes),
        out_shape=(out, out),
        in_specs=[vmem] * 3,
        out_specs=(vmem, vmem),
        scratch_shapes=[
            pltpu.VMEM((nodes, layers, width), F32),
            pltpu.VMEM((layers, width), F32),
            pltpu.VMEM((layers, width), F32),
            pltpu.VMEM((nodes,) + tile, F32),
            pltpu.VMEM((span,) + tile, F32),
            pltpu.VMEM((nodes,) + tile, F32),
            pltpu.VMEM((N * 16,) + tile, F32),
            pltpu.VMEM((12,) + tile, F32),
            pltpu.VMEM((2 * REACH,) + tile, F32),
            pltpu.VMEM((2, 16) + tile, F32),
            pltpu.VMEM((2, messages) + tile, F32),
            pltpu.VMEM((2, 2, messages) + tile, F32),
            pltpu.VMEM((CYCLES, span, 2) + tile, F32),
            dma((2,)), dma((2,)), dma((span,)), dma((span,)),
            dma((2,)), dma((2, 2)), dma((span,)), dma((CYCLES, span)),
        ],
        compiler_params=pltpu.CompilerParams(collective_id=0, has_side_effects=True),
    )(load.reshape(nodes, layers, width), kappa.reshape(layers, width), wet.reshape(layers, width))
    return solution.reshape(load.shape), residual.reshape(load.shape)


def solution(mesh):
    sizes = tuple(mesh.shape[name] for name in ("ex", "ey", "lin"))
    field = P(None, None, None, None, ("ey", "lin"), "ex")
    cell = P(None, ("ey", "lin"), "ex")
    return jax.shard_map(
        functools.partial(per_device, sizes), mesh=mesh, in_specs=(field, cell, cell),
        out_specs=(field, field), check_vma=False,
    )
```

```python
import functools
import math

import jax
import jax.numpy as jnp
import numpy as np
from jax import lax
from jax.experimental import pallas as pl
from jax.experimental.pallas import tpu as pltpu
from jax.sharding import PartitionSpec as P

N = 5
CYCLES = 2
NPRE = 2
NPOST = 2
NC = 4
FINE_RELAX = 0.25
COARSE_RELAX = 0.4
REACH = NC + 1
STEPS = CYCLES * (NPRE + NPOST) + 1
HALO = 32
MESH = pl.DeviceIdType.MESH
F32 = jnp.float32


def node_tables():
    points = np.array([-1.0, -math.sqrt(3.0 / 7.0), 0.0, math.sqrt(3.0 / 7.0), 1.0])
    weights = np.array([0.1, 49.0 / 90.0, 32.0 / 45.0, 49.0 / 90.0, 0.1])
    eye_table = np.eye(points.shape[0])
    spread = points[:, None] - points[None, :] + eye_table
    factors = np.prod(spread, axis=1)
    deriv = factors[:, None] / (factors[None, :] * spread)
    deriv = np.where(eye_table > 0, (np.sum(1.0 / spread, axis=1) - 1.0)[:, None], deriv)
    stiff = deriv.T @ (weights[:, None] * deriv)
    mass = eye_table * weights[:, None]
    interp = np.stack([(1.0 - points) / 2.0, (1.0 + points) / 2.0], axis=1)
    return stiff, weights, interp, interp.T @ stiff @ interp, interp.T @ mass @ interp


STIFF, WEIGHTS, INTERP, COARSE_STIFF, COARSE_MASS = node_tables()
D = STIFF / WEIGHTS[:, None]
W3 = WEIGHTS[:, None, None] * WEIGHTS[None, :, None] * WEIGHTS[None, None, :]
DD = np.diag(D)
K3 = W3 * (DD[:, None, None] + DD[None, :, None] + DD[None, None, :])


def node(a, b, c):
    return (a * N + b) * N + c


def line_parts(v):
    twice = v[2] + v[2]
    return (v[0] + v[4]) - twice, (v[1] + v[3]) - twice, v[0] - v[4], v[1] - v[3]


def row_even(i, parts):
    return float((D[i, 0] + D[i, 4]) / 2) * parts[0] + float((D[i, 1] + D[i, 3]) / 2) * parts[1]


def row_odd(i, parts):
    return float((D[i, 0] - D[i, 4]) / 2) * parts[2] + float((D[i, 1] - D[i, 3]) / 2) * parts[3]


def line_apply(v):
    parts = line_parts(v)
    e0, e1, e2 = (row_even(i, parts) for i in range(3))
    o0, o1 = (row_odd(i, parts) for i in range(2))
    return [e0 + o0, e1 + o1, e2, e1 - o1, e0 - o0]


def scaled(factor, value):
    factor = float(factor)
    if factor == 1.0:
        return value
    return factor * value


def mix(pairs):
    total = None
    for factor, value in pairs:
        if abs(float(factor)) < 1e-14:
            continue
        term = scaled(factor, value)
        total = term if total is None else total + term
    return total


def kernel(
    sizes, load_ref, kappa_ref, wet_ref, sol_out, res_out,
    other_load, other_coeff, own_coeff, load, coeffs, sol, total, inverse, cinv, face, packed, got, cgot,
    ex_send, ex_recv, k_send, k_recv, f_send, f_recv, c_send, c_recv,
):
    ex_count, ey_count, lin_count, layers, width = sizes
    ex, ey, lin = lax.axis_index("ex"), lax.axis_index("ey"), lax.axis_index("lin")
    rows = ey_count * lin_count
    row = ey * lin_count + lin
    own = REACH

    sub = lax.broadcasted_iota(jnp.int32, (2 * layers, width), 0)
    lane = lax.broadcasted_iota(jnp.int32, (2 * layers, width), 1)
    layer = sub % layers
    bottom, top = layer == 0, layer == layers - 1
    first_lane, last_lane = lane == 0, lane == width - 1
    near = jnp.where(ex == 0, lane, width - 1 - lane)
    real = (sub < layers) | (near < HALO)

    def like(mask, x):
        return jnp.broadcast_to(mask, x.shape) if x.ndim == 3 else mask

    def before(x):
        y = pltpu.roll(x, 1, x.ndim - 1)
        return jnp.where(like(first_lane, x), pltpu.roll(y, layers, x.ndim - 2), y)

    def after(x):
        y = pltpu.roll(x, width - 1, x.ndim - 1)
        return jnp.where(like(last_lane, x), pltpu.roll(y, layers, x.ndim - 2), y)

    def below(low, high):
        return jnp.where(like(bottom, low), low, low + pltpu.roll(high, 1, low.ndim - 2))

    def above(low):
        return jnp.where(like(top, low), 0.0, pltpu.roll(low, 2 * layers - 1, low.ndim - 2))

    def place(at):
        return (ex, at // lin_count, at % lin_count)

    def partners(fn):
        for d in range(1, REACH + 1):
            @pl.when(row >= d)
            def _():
                fn(row - d, own + d, own - d)

            @pl.when(row + d < rows)
            def _():
                fn(row + d, own - d, own + d)

    coeffs[...] = jnp.zeros_like(coeffs)
    cgot[...] = jnp.zeros_like(cgot)
    got[...] = jnp.zeros_like(got)
    barrier = pltpu.get_barrier_semaphore()
    pl.semaphore_signal(barrier, inc=1, device_id=(1 - ex, ey, lin), device_id_type=MESH)
    partners(lambda at, theirs, mine: pl.semaphore_signal(
        barrier, inc=1, device_id=place(at), device_id_type=MESH))

    coeff_own = kappa_ref[...] * jnp.where(wet_ref[...] == 1, F32(1.0), F32(0.05))
    own_coeff[...] = coeff_own

    pl.semaphore_wait(barrier, 1 + jnp.minimum(row, REACH) + jnp.minimum(rows - 1 - row, REACH))

    def ex_copy(src, dst, i):
        return pltpu.make_async_remote_copy(
            src_ref=src, dst_ref=dst, send_sem=ex_send.at[i], recv_sem=ex_recv.at[i],
            device_id=(1 - ex, ey, lin), device_id_type=MESH)

    coeff_copy = ex_copy(own_coeff, other_coeff, 0)
    load_copy = ex_copy(load_ref, other_load, 1)
    coeff_copy.start()
    load_copy.start()
    sol[...] = jnp.zeros_like(sol)
    coeff_copy.wait()
    coeffs[own] = jnp.where(real, jnp.concatenate([coeff_own, other_coeff[...]], axis=0), 0.0)

    def k_copy(at, theirs, mine):
        return pltpu.make_async_remote_copy(
            src_ref=coeffs.at[own], dst_ref=coeffs.at[theirs],
            send_sem=k_send.at[mine], recv_sem=k_recv.at[theirs],
            device_id=place(at), device_id_type=MESH)

    def k_wait(at, theirs, mine):
        pltpu.make_async_remote_copy(
            src_ref=coeffs.at[own], dst_ref=coeffs.at[mine],
            send_sem=k_send.at[mine], recv_sem=k_recv.at[mine],
            device_id=place(at), device_id_type=MESH).wait()

    partners(lambda *p: k_copy(*p).start())
    load_copy.wait()

    def join(i, _):
        for k in range(N * N):
            at = i * N * N + k
            load[at] = jnp.where(real, jnp.concatenate([load_ref[at], other_load[at]], axis=0), 0.0)
        return 0

    lax.fori_loop(0, N, join, 0)
    def inverted(x):
        return jnp.where(x > 0.0, 1.0 / jnp.where(x > 0.0, x, 1.0), 0.0)

    def invert():
        partners(k_wait)
        here = coeffs[own]
        for kind, x in enumerate((here, here + coeffs[own - 1], here + coeffs[own + 1])):
            xc = x + before(x)
            for slot, y in enumerate((x, xc, below(x, x), below(xc, xc))):
                inverse[kind * 4 + slot] = inverted(y)
        pairs = coeffs[0:2 * REACH] + coeffs[1:2 * REACH + 1]
        pairs = pairs + before(pairs)
        pairs = below(pairs, pairs)
        corner = 3.0 * COARSE_STIFF[0, 0] * COARSE_MASS[0, 0] ** 2
        cinv[...] = float(COARSE_RELAX / corner) * inverted(pairs)

    def plane_local(b):
        v = [[sol[node(a, b, c)] for c in range(N)] for a in range(N)]
        acc = [line_apply(v[a]) for a in range(N)]
        for c in range(N):
            column = line_apply([v[a][c] for a in range(N)])
            for a in range(N):
                acc[a][c] = acc[a][c] + column[a]
        coeff = coeffs[own]
        out = []
        for a in range(N):
            line = []
            for c in range(N):
                parts = line_parts([sol[node(a, k, c)] for k in range(N)])
                side = min(b, N - 1 - b)
                term = row_even(side, parts)
                if b < 2:
                    term = term + row_odd(side, parts)
                elif b > 2:
                    term = term - row_odd(side, parts)
                value = acc[a][c] + term
                line.append(load[node(a, b, c)] - float(W3[a, b, c]) * coeff * value)
            out.append(line)
        return out

    def gather_plane(f):
        h = []
        for a in range(N):
            h.append([f[a][0] + before(f[a][N - 1])] + f[a][1:N - 1])
        return [[below(h[0][c], h[N - 1][c]) for c in range(N - 1)]] + h[1:N - 1]

    def put_plane(b, values, ref):
        for a in range(N - 1):
            line = list(values[a])
            line.append(after(line[0]))
            for c in range(N):
                ref[node(a, b, c)] = line[c]
                if a == 0:
                    ref[node(N - 1, b, c)] = above(line[c])

    def update_plane(b, scale):
        kind = 0 if 0 < b < N - 1 else (1 if b == 0 else 2)
        values = []
        for a in range(N - 1):
            line = []
            for c in range(N - 1):
                inv = inverse[kind * 4 + (2 if a == 0 else 0) + (1 if c == 0 else 0)] * scale
                line.append(sol[node(a, b, c)] + float(FINE_RELAX / K3[a, b, c]) * inv * total[(b * 4 + a) * 4 + c])
            values.append(line)
        put_plane(b, values, sol)

    def c_copy(cycle, at, theirs, mine):
        return pltpu.make_async_remote_copy(
            src_ref=cgot.at[cycle, own], dst_ref=cgot.at[cycle, theirs],
            send_sem=c_send.at[mine], recv_sem=c_recv.at[cycle, theirs],
            device_id=place(at), device_id_type=MESH)

    def c_wait(cycle, at, theirs, mine):
        pltpu.make_async_remote_copy(
            src_ref=cgot.at[cycle, own], dst_ref=cgot.at[cycle, mine],
            send_sem=c_send.at[mine], recv_sem=c_recv.at[cycle, mine],
            device_id=place(at), device_id_type=MESH).wait()

    def gather(q, j):
        h = [q[i, j, 0] + before(q[i, j, 1]) for i in range(2)]
        return below(h[0], h[1])

    def coarse_send(cycle):
        q = {}
        for b in range(N):
            side = {0: 0, N - 1: 1}.get(b)
            f = [[total[(b * 4 + a) * 4 + c] if side is None else face[side, a * 4 + c]
                  for c in range(N - 1)] for a in range(N - 1)]
            g = [[mix((INTERP[c, k], f[a][c]) for c in range(N - 1)) for k in range(2)] for a in range(N - 1)]
            for i in range(2):
                for k in range(2):
                    h = mix((INTERP[a, i], g[a][k]) for a in range(N - 1))
                    for j in range(2):
                        if INTERP[b, j] != 0:
                            term = scaled(INTERP[b, j], h)
                            q[i, j, k] = q[i, j, k] + term if (i, j, k) in q else term
        for j in range(2):
            cgot[cycle, own, j] = gather(q, j)
        partners(lambda *p: c_copy(cycle, *p).start())

    def correct(cycle):
        partners(lambda *p: c_wait(cycle, *p))
        lines = 2 * REACH
        rc = cgot[cycle, 0:lines, 1] + cgot[cycle, 1:lines + 1, 0]
        inv = cinv[...]
        correction = inv * rc
        coeff = coeffs[1:lines]

        def corners(x):
            right = after(x)
            return {(0, 0): x, (0, 1): right, (1, 0): above(x), (1, 1): above(right)}

        def two(m, x, y):
            return [mix(((m[p, 0], x), (m[p, 1], y))) for p in range(2)]

        for sweep in range(NC - 1):
            nodes = corners(correction)
            v = {(i, j, k): nodes[i, k][j:j + lines - 1] for i in range(2) for j in range(2) for k in range(2)}

            def along(m, v, axis):
                out = {}
                for x in range(2):
                    for y in range(2):
                        key = [(0, x, y), (x, 0, y), (x, y, 0)][axis]
                        key1 = [(1, x, y), (x, 1, y), (x, y, 1)][axis]
                        out[key], out[key1] = two(m, v[key], v[key1])
                return out

            mc = along(COARSE_MASS, v, 2)
            first = along(COARSE_STIFF, along(COARSE_MASS, mc, 1), 0)
            rest = along(COARSE_STIFF, mc, 1)
            third = along(COARSE_MASS, along(COARSE_STIFF, v, 2), 1)
            rest = along(COARSE_MASS, {key: rest[key] + third[key] for key in rest}, 0)
            q2 = {key: coeff * (first[key] + rest[key]) for key in rest}
            low, high = gather(q2, 0), gather(q2, 1)
            zero = jnp.zeros_like(low[0:1])
            image = jnp.concatenate([low, zero], axis=0) + jnp.concatenate([zero, high], axis=0)
            correction = correction + inv * (rc - image)
        ends = [corners(correction[own - 2 + m]) for m in range(4)]

        def interpolated(k, b):
            return {key: mix(((INTERP[b, j], ends[k + j][key]) for j in range(2))) for key in ends[0]}

        def operated(k, b):
            coeff = coeffs[own - 1 + k]
            half = {key: (0.5 * coeff) * value for key, value in interpolated(k, b).items()}
            f = [[None] * N for _ in range(N)]

            def put(a, c, value):
                f[a][c] = value if f[a][c] is None else f[a][c] + value

            rise_c = [half[i, 1] - half[i, 0] for i in range(2)]
            rise_a = [half[1, i] - half[0, i] for i in range(2)]
            for n in range(N):
                value = float(WEIGHTS[n] * WEIGHTS[b]) * mix(((INTERP[n, i], rise_c[i]) for i in range(2)))
                put(n, 0, value)
                put(n, N - 1, -value)
                value = float(WEIGHTS[n] * WEIGHTS[b]) * mix(((INTERP[n, i], rise_a[i]) for i in range(2)))
                put(0, n, value)
                put(N - 1, n, -value)
            if b in (0, N - 1):
                sign = 0.5 if b == 0 else -0.5
                rise_b = {key: (sign * coeff) * (ends[k + 1][key] - ends[k][key]) for key in ends[0]}
                for a in range(N):
                    pair = [mix(((INTERP[a, i], rise_b[i, x]) for i in range(2))) for x in range(2)]
                    for c in range(N):
                        put(a, c, float(WEIGHTS[a] * WEIGHTS[c]) * mix(((INTERP[c, x], pair[x]) for x in range(2))))
            return f

        for b in range(N):
            sums = [gather_plane(operated(1, b))]
            if b == 0:
                sums.append(gather_plane(operated(0, N - 1)))
            if b == N - 1:
                sums.append(gather_plane(operated(2, 0)))
            mid = interpolated(1, b)
            for a in range(N - 1):
                pair = [mix(((INTERP[a, i], mid[i, k]) for i in range(2))) for k in range(2)]
                for c in range(N - 1):
                    at = node(a, b, c)
                    sol[at] = sol[at] + mix(((INTERP[c, k], pair[k]) for k in range(2)))
                    if sums[0][a][c] is not None:
                        at = (b * 4 + a) * 4 + c
                        value = total[at]
                        for one in sums:
                            value = value + one[a][c]
                        total[at] = value

    fold = width // HALO
    block = lax.rem(lane + jnp.where(ex == 0, 0, HALO - 1), width) // HALO
    lower = sub < layers

    def swap(x):
        return pltpu.roll(x, layers, 0)

    def pack(side, x):
        for p in range(8):
            packed[side, p] = jnp.where(lower, x[2 * p], swap(x[2 * p + 1]))
        for p in range(8 // fold):
            halves = []
            for h in range(2):
                group = x[(2 * p + h) * fold:(2 * p + h + 1) * fold]
                mixed = group[0]
                for j in range(1, fold):
                    mixed = jnp.where(block == j, pltpu.roll(group[j], HALO * j, 1), mixed)
                halves.append(mixed)
            packed[side, 8 + p] = jnp.where(lower, swap(halves[0]), halves[1])

    def unpack(slot, side):
        x = []
        for p in range(8 // fold):
            tile = got[slot, side, 8 + p]
            for half in (swap(tile), tile):
                for j in range(fold):
                    other = half if j == 0 else pltpu.roll(half, width - HALO * j, 1)
                    n = len(x)
                    mine = got[slot, side, n // 2]
                    mine = mine if n % 2 == 0 else swap(mine)
                    x.append(jnp.where(lower, mine, jnp.where(block == 0, other, 0.0)))
        return x

    def face_copy(slot, side, at):
        return pltpu.make_async_remote_copy(
            src_ref=packed.at[side], dst_ref=got.at[slot, 1 - side],
            send_sem=f_send.at[side], recv_sem=f_recv.at[slot, 1 - side],
            device_id=place(at), device_id_type=MESH)

    def face_wait(slot, side, at):
        pltpu.make_async_remote_copy(
            src_ref=packed.at[side], dst_ref=got.at[slot, side],
            send_sem=f_send.at[side], recv_sem=f_recv.at[slot, side],
            device_id=place(at), device_id_type=MESH).wait()

    def both(fn):
        @pl.when(row >= 1)
        def _():
            fn(0, row - 1)

        @pl.when(row + 1 < rows)
        def _():
            fn(1, row + 1)

    def step(s, _):
        slot = lax.rem(s, 2)

        cycle = s // (NPRE + NPOST)
        coarse = (lax.rem(s, NPRE + NPOST) == NPRE) & (s < STEPS - 1)

        for side in range(2):
            summed = gather_plane(plane_local(side * (N - 1)))
            for a in range(N - 1):
                for c in range(N - 1):
                    face[side, a * 4 + c] = summed[a][c]
            pack(side, [value for values in summed for value in values])
        both(lambda side, at: face_copy(slot, side, at).start())
        for b in range(1, N - 1):
            summed = gather_plane(plane_local(b))
            for a in range(N - 1):
                for c in range(N - 1):
                    total[(b * 4 + a) * 4 + c] = summed[a][c]
        scale = jnp.where(s < STEPS - 1, F32(1.0), F32(0.0))

        @pl.when(s == 0)
        def _():
            invert()

        @pl.when(coarse)
        def _():
            coarse_send(cycle)

        @pl.when(jnp.logical_not(coarse))
        def _():
            for b in range(1, N - 1):
                update_plane(b, scale)

        both(lambda side, at: face_wait(slot, side, at))
        for side in range(2):
            theirs = unpack(slot, side)
            for i in range(16):
                total[side * (N - 1) * 16 + i] = face[side, i] + theirs[i]

        @pl.when(coarse)
        def _():
            correct(cycle)
            for b in range(1, N - 1):
                update_plane(b, scale)

        for side in range(2):
            update_plane(side * (N - 1), scale)
        return 0

    lax.fori_loop(0, STEPS, step, 0)

    for b in range(N):
        put_plane(b, [[total[(b * 4 + a) * 4 + c] for c in range(N - 1)] for a in range(N - 1)], load)

    def out(i, _):
        for k in range(N * N):
            at = i * N * N + k
            sol_out[at] = sol[at][0:layers]
            res_out[at] = load[at][0:layers]
        return 0

    lax.fori_loop(0, N, out, 0)


def per_device(sizes, load, kappa, wet):
    layers, _, width = kappa.shape
    nodes = N * N * N
    tile = (2 * layers, width)
    sizes = sizes + (layers, width)
    out = jax.ShapeDtypeStruct((nodes, layers, width), F32)
    vmem = pl.BlockSpec(memory_space=pltpu.VMEM)
    span = 2 * REACH + 1
    messages = 8 + 8 * HALO // width
    dma = pltpu.SemaphoreType.DMA
    solution, residual = pl.pallas_call(
        functools.partial(kernel, sizes),
        out_shape=(out, out),
        in_specs=[vmem] * 3,
        out_specs=(vmem, vmem),
        scratch_shapes=[
            pltpu.VMEM((nodes, layers, width), F32),
            pltpu.VMEM((layers, width), F32),
            pltpu.VMEM((layers, width), F32),
            pltpu.VMEM((nodes,) + tile, F32),
            pltpu.VMEM((span,) + tile, F32),
            pltpu.VMEM((nodes,) + tile, F32),
            pltpu.VMEM((N * 16,) + tile, F32),
            pltpu.VMEM((12,) + tile, F32),
            pltpu.VMEM((2 * REACH,) + tile, F32),
            pltpu.VMEM((2, 16) + tile, F32),
            pltpu.VMEM((2, messages) + tile, F32),
            pltpu.VMEM((2, 2, messages) + tile, F32),
            pltpu.VMEM((CYCLES, span, 2) + tile, F32),
            dma((2,)), dma((2,)), dma((span,)), dma((span,)),
            dma((2,)), dma((2, 2)), dma((span,)), dma((CYCLES, span)),
        ],
        compiler_params=pltpu.CompilerParams(collective_id=0, has_side_effects=True),
    )(load.reshape(nodes, layers, width), kappa.reshape(layers, width), wet.reshape(layers, width))
    return solution.reshape(load.shape), residual.reshape(load.shape)


def solution(mesh):
    sizes = tuple(mesh.shape[name] for name in ("ex", "ey", "lin"))
    field = P(None, None, None, None, ("ey", "lin"), "ex")
    cell = P(None, ("ey", "lin"), "ex")
    return jax.shard_map(
        functools.partial(per_device, sizes), mesh=mesh, in_specs=(field, cell, cell),
        out_specs=(field, field), check_vma=False,
    )
```
